512 devices in a mesh: fsdp: 32 (over y, z_lo), ex: 16 (over x, z_hi, core).
Axes of the slice: x: 4, y: 8, z: 8 (z_hi: 2, z_lo: 4; z = z_hi * 4 + z_lo), core: 2. Of those that a mesh axis runs over, the one named last changes fastest.
Arguments:
- activations: bfloat16 [65536, 4096], P('ex', 'fsdp'), may hold values from -6 to 6
- out_grads: bfloat16 [65536, 11008], P('ex', 'fsdp'), may hold values from -6 to 6
- in_factor: bfloat16 [4096, 64], P('fsdp'), may hold values from -0.09375 to 0.09375
- out_factor: bfloat16 [11008, 32], P('fsdp'), may hold values from -0.0546875 to 0.0546875
- test_features: float32 [512, 2048], P('fsdp'), may hold values from -6 to 6
Outputs:
- kernel: float32 [2048, 2048], P('fsdp', 'ex')
- scores: float32 [512, 64], P('fsdp', 'ex')
The draws below stay inside these ranges and needn't reach their ends.
All inputs are finite; a program needn't handle non-finite values.
Results may differ from the reference program's by a relative error of at most 0.0003.
Values sent between devices are 32-bit elements; how exact they have to be, the bound alone decides.
No kernel may reach another device: no remote copies, remote signals or barrier semaphores. Data moves between devices by JAX's collectives and lax.ppermute only.
A program may use at most 64 MiB of HBM per device.

```python
import math
import jax
import jax.numpy as jnp
from jax import lax

D_IN = 4096
D_OUT = 11008
K_IN = 64
K_OUT = 32
LEN = 1024
FEAT = 2048
N_TRAIN = 64
N_TEST = 512
ROWS = 65536


def block_scale(rng, shape, split, least, high):
    level = 1.0
    for axis_at, shards_of in split:
        heights = jax.random.uniform(jax.random.fold_in(jax.random.fold_in(rng, 6), axis_at), (shards_of,), jnp.float32, least / len(split), high / len(split))
        level = level * jnp.repeat(jnp.exp(heights), shape[axis_at] // shards_of).reshape((-1,) + (1,) * (len(shape) - 1 - axis_at))
    return level


def noise(own_key, shape, scale, bound, cuts=(), kind=jnp.bfloat16):
    level = block_scale(own_key, shape, cuts, -0.22, 0.18) if cuts else 1.0
    array = jax.random.normal(own_key, shape, jnp.float32) * scale * level
    return jnp.minimum(jnp.maximum(array, -bound), bound).astype(kind)


def setup_inputs(seed: int = 0) -> dict:
    seeds = jax.random.split(jax.random.key(seed), 6)
    activations = noise(seeds[0], (ROWS, D_IN), 1.0, 6.0, ((0, 16), (1, 32)))
    out_grads = noise(seeds[1], (ROWS, D_OUT), 1.0, 6.0, ((0, 16), (1, 32)))
    in_factor = noise(seeds[2], (D_IN, K_IN), D_IN ** -0.5, 0.09375, ((0, 32),))
    out_factor = noise(seeds[3], (D_OUT, K_OUT), D_OUT ** -0.5, 0.0546875, ((0, 32),))
    test_features = noise(seeds[4], (N_TEST, FEAT), 1.0, 6.0, ((0, 32),), jnp.float32)
    return dict(activations=activations, out_grads=out_grads, in_factor=in_factor, out_factor=out_factor, test_features=test_features)


def reference(activations, out_grads, in_factor, out_factor, test_features):
    in_wide = in_factor.astype(jnp.float32)
    out_wide = out_factor.astype(jnp.float32)

    def featurize(example):
        first_row = (example * LEN).astype(jnp.int32)
        act_rows = lax.dynamic_slice_in_dim(activations, first_row, LEN, 0).astype(jnp.float32)
        grad_rows = lax.dynamic_slice_in_dim(out_grads, first_row, LEN, 0).astype(jnp.float32)
        proj_in = jnp.dot(act_rows, in_wide, precision=lax.Precision.HIGHEST)
        proj_out = jnp.dot(grad_rows, out_wide, precision=lax.Precision.HIGHEST)
        outer_sum = jnp.dot(proj_in.T, proj_out, precision=lax.Precision.HIGHEST)
        return outer_sum.reshape(FEAT) / math.sqrt(LEN)
    features = lax.map(featurize, jnp.arange(N_TRAIN, dtype=jnp.int32))
    kernel = jnp.dot(features.T, features, precision=lax.Precision.HIGHEST) / N_TRAIN + jnp.eye(FEAT, dtype=jnp.float32)
    scores = jnp.dot(test_features, features.T, precision=lax.Precision.HIGHEST) / math.sqrt(FEAT)
    return (kernel, scores)
```

```python
import functools
import math

import jax
import jax.numpy as jnp
from jax import lax
from jax.experimental import pallas as pl
from jax.experimental.pallas import tpu as pltpu
from jax.sharding import PartitionSpec as P

LEN = 1024
LANES = 128
HIGHEST = lax.Precision.HIGHEST
VMEM = pl.BlockSpec(memory_space=pltpu.VMEM)


def nt_dot(a, b, **kw):
    return lax.dot_general(a, b, (((1,), (1,)), ((), ())), preferred_element_type=jnp.float32, **kw)


def project_kernel(act_ref, grad_t_ref, in_t_ref, out_t_ref, chunk_ref):
    in_rank = in_t_ref.shape[0]
    proj_in = nt_dot(in_t_ref[...], act_ref[...])
    proj_out = jnp.dot(out_t_ref[...], grad_t_ref[...], preferred_element_type=jnp.float32)
    for s in range(chunk_ref.shape[0]):
        cols = slice(s * LANES, (s + 1) * LANES)
        chunk_ref[s, :in_rank, :] = proj_in[:, cols]
        chunk_ref[s, in_rank:, :] = proj_out[:, cols]


def outer_kernel(in_rank, parts_ref, out_ref, sum_ref):
    total = parts_ref[0]
    for s in range(1, parts_ref.shape[0]):
        total = total + parts_ref[s]
    sum_ref[...] = total
    out_rank = total.shape[0] - in_rank
    per_row = LANES // out_rank
    rows = in_rank // per_row
    proj_in = jnp.concatenate(
        [sum_ref[pl.ds(a, rows, stride=per_row), :] for a in range(per_row)], axis=0
    )
    proj_out = jnp.concatenate([total[in_rank:]] * per_row, axis=0)
    full = nt_dot(proj_in, proj_out, precision=HIGHEST)
    group = lax.broadcasted_iota(jnp.int32, (rows, LANES), 1) // out_rank
    dense = full[:rows]
    for a in range(1, per_row):
        dense = jnp.where(group == a, full[a * rows : (a + 1) * rows], dense)
    out_ref[...] = jnp.broadcast_to(dense[None], out_ref.shape)


def scores_kernel(factor_scale, score_scale, parts_ref, test_ref, send_ref, scores_ref, phi_ref):
    sources, rows, _ = parts_ref.shape
    ex_dev = scores_ref.shape[0]
    slices = sources // ex_dev
    tests = test_ref.shape[0]
    weighted = []
    for x in range(ex_dev):
        phi = parts_ref[x * slices]
        for s in range(1, slices):
            phi = phi + parts_ref[x * slices + s]
        phi = phi * factor_scale
        phi_ref[x * rows : (x + 1) * rows, :] = phi
        acc = jnp.zeros((tests, LANES), jnp.float32)
        for r in range(rows):
            acc = acc + test_ref[:, r * LANES : (r + 1) * LANES] * phi[r : r + 1, :]
        weighted.append(acc)
    ones = jnp.ones((8, LANES), jnp.float32)
    sums = nt_dot(ones, jnp.concatenate(weighted, axis=0), precision=HIGHEST) * score_scale
    for x in range(ex_dev):
        scores_ref[x : x + 1, :] = sums[0:1, x * tests : (x + 1) * tests]
    me = lax.axis_index("fsdp")
    own = phi_ref[pl.ds(me // 2, ex_dev, stride=rows), :]
    own = jnp.where(me % 2 == 0, own, pltpu.roll(own, LANES // 2, 1))
    for r in range(rows):
        send_ref[r, :ex_dev, :] = phi_ref[pl.ds(r, ex_dev, stride=rows), :]
        send_ref[r, ex_dev:, :] = own


def tile_kernel(ex_all, recv_ref, out_ref):
    groups, both, _ = recv_ref.shape
    half = both // 2
    recv = recv_ref[...]
    first = lax.broadcasted_iota(jnp.int32, recv.shape, 1) < half
    cols = jnp.where(first, recv, 0.0).reshape(groups * both, LANES)
    swapped = jnp.concatenate([recv[:, half:], recv[:, :half]], axis=1)
    rows = jnp.where(first, swapped, 0.0).reshape(groups * both, LANES)
    tile = lax.dot_general(
        rows, cols, (((0,), (0,)), ((), ())), preferred_element_type=jnp.float32, precision=HIGHEST
    )
    height = out_ref.shape[0]
    row_start = lax.axis_index("fsdp") * height
    col_start = lax.axis_index("ex") * LANES
    row_index = row_start + lax.broadcasted_iota(jnp.int32, out_ref.shape, 0)
    col_index = col_start + lax.broadcasted_iota(jnp.int32, out_ref.shape, 1)
    eye = jnp.where(row_index == col_index, 1.0, 0.0).astype(jnp.float32)
    out_ref[...] = tile[:height] * (1.0 / ex_all) + eye


def shards(activations, out_grads, in_factor, out_factor, test_features):
    fsdp_count = lax.axis_size("fsdp")
    ex_count = lax.axis_size("ex")
    rows_total, in_width = activations.shape
    out_width = out_grads.shape[1]
    in_rank = in_factor.shape[1]
    out_rank = out_factor.shape[1]
    rank = in_rank + out_rank
    features = in_rank * out_rank
    ex_dev = rows_total // LEN
    tests = test_features.shape[0]
    feature_rows = features // LANES
    steps = 4
    block = rows_total // steps
    f32 = jnp.float32

    chunks = pl.pallas_call(
        project_kernel,
        grid=(steps,),
        in_specs=[
            pl.BlockSpec((block, in_width), lambda i: (i, 0)),
            pl.BlockSpec((out_width, block), lambda i: (0, i)),
            pl.BlockSpec((in_rank, in_width), lambda i: (0, 0)),
            pl.BlockSpec((out_rank, out_width), lambda i: (0, 0)),
        ],
        out_specs=pl.BlockSpec((block // LANES, rank, LANES), lambda i: (i, 0, 0)),
        out_shape=jax.ShapeDtypeStruct((fsdp_count, rank, LANES), f32),
        name="project",
    )(activations, out_grads.T, in_factor.T, out_factor.T)
    parts = lax.all_to_all(chunks, "fsdp", 0, 0, tiled=True)

    outer = pl.pallas_call(
        functools.partial(outer_kernel, in_rank),
        in_specs=[VMEM],
        out_specs=VMEM,
        out_shape=jax.ShapeDtypeStruct((fsdp_count, feature_rows, LANES), f32),
        scratch_shapes=[pltpu.VMEM((rank, LANES), f32)],
        name="outer",
    )(parts)
    partials = lax.all_to_all(outer, "fsdp", 0, 0, tiled=True)

    send, scores_t = pl.pallas_call(
        functools.partial(scores_kernel, 1.0 / math.sqrt(LEN), 1.0 / math.sqrt(features)),
        in_specs=[VMEM, VMEM],
        out_specs=[VMEM, VMEM],
        out_shape=[
            jax.ShapeDtypeStruct((ex_count, 2 * ex_dev, LANES), f32),
            jax.ShapeDtypeStruct((ex_dev, tests), f32),
        ],
        scratch_shapes=[pltpu.VMEM((ex_dev * feature_rows, LANES), f32)],
        name="scores",
    )(partials, test_features)
    recv = lax.all_to_all(send, "ex", 0, 0, tiled=True)

    kernel = pl.pallas_call(
        functools.partial(tile_kernel, ex_dev * ex_count),
        in_specs=[VMEM],
        out_specs=VMEM,
        out_shape=jax.ShapeDtypeStruct((features // fsdp_count, features // ex_count), f32),
        name="tile",
    )(recv)
    return (kernel, scores_t.T)


def solution(mesh):
    in_specs = (P("ex", "fsdp"), P("ex", "fsdp"), P("fsdp", None), P("fsdp", None), P("fsdp", None))
    out_specs = (P("fsdp", "ex"), P("fsdp", "ex"))
    return jax.shard_map(shards, mesh=mesh, in_specs=in_specs, out_specs=out_specs, check_vma=False)
```

```python
import functools
import math

import jax
import jax.numpy as jnp
from jax import lax
from jax.experimental import pallas as pl
from jax.experimental.pallas import tpu as pltpu
from jax.sharding import PartitionSpec as P

LEN = 1024
LANES = 128
Z = 4
LIMIT = pltpu.CompilerParams(vmem_limit_bytes=16 * 2**20)
HIGHEST = lax.Precision.HIGHEST
VMEM = pl.BlockSpec(memory_space=pltpu.VMEM)


def nt_dot(a, b, **kw):
    return lax.dot_general(a, b, (((1,), (1,)), ((), ())), preferred_element_type=jnp.float32, **kw)


def project_kernel(act_ref, grad_t_ref, in_t_ref, out_t_ref, chunk_ref):
    in_rank = in_t_ref.shape[0]
    proj_in = nt_dot(in_t_ref[...], act_ref[...])
    proj_out = jnp.dot(out_t_ref[...], grad_t_ref[...], preferred_element_type=jnp.float32)
    for s in range(chunk_ref.shape[0]):
        cols = slice(s * LANES, (s + 1) * LANES)
        chunk_ref[s, :in_rank, :] = proj_in[:, cols]
        chunk_ref[s, in_rank:, :] = proj_out[:, cols]


def block_groups(fsdp_count):
    blocks = range(fsdp_count // Z // 2)
    place = lambda y, z, dy, dz: (2 * y + dy) * Z + 2 * z + dz
    pair, halves = range(2), range(Z // 2)
    near = [[place(y, z, dy, dz) for dy in pair for dz in pair] for y in blocks for z in halves]
    far = [[place(y, z, dy, dz) for y in blocks for z in halves] for dy in pair for dz in pair]
    return near, far


def sum_kernel(parts_ref, out_ref):
    total = parts_ref[0]
    for s in range(1, parts_ref.shape[0]):
        total = total + parts_ref[s]
    out_ref[...] = total


def outer_kernel(in_rank, parts_ref, out_ref, sum_ref):
    total = parts_ref[0]
    for s in range(1, parts_ref.shape[0]):
        total = total + parts_ref[s]
    sum_ref[...] = total
    out_rank = total.shape[0] - in_rank
    per_row = LANES // out_rank
    rows = in_rank // per_row
    proj_in = jnp.concatenate(
        [sum_ref[pl.ds(a, rows, stride=per_row), :] for a in range(per_row)], axis=0
    )
    proj_out = jnp.concatenate([total[in_rank:]] * per_row, axis=0)
    full = nt_dot(proj_in, proj_out, precision=HIGHEST)
    group = lax.broadcasted_iota(jnp.int32, (rows, LANES), 1) // out_rank
    dense = full[:rows]
    for a in range(1, per_row):
        dense = jnp.where(group == a, full[a * rows : (a + 1) * rows], dense)
    out_ref[...] = jnp.broadcast_to(dense[None], out_ref.shape)


def scores_kernel(factor_scale, score_scale, parts_ref, test_ref, send_ref, scores_ref, phi_ref):
    sources, rows, _ = parts_ref.shape
    ex_dev = scores_ref.shape[0]
    near = lambda f: f // Z % 2 * 2 + f % 2
    tests = test_ref.shape[0]
    weighted = []
    for x in range(ex_dev):
        phi = sum(parts_ref[f] for f in range(sources) if near(f) == x) * factor_scale
        phi_ref[x * rows : (x + 1) * rows, :] = phi
        acc = jnp.zeros((tests, LANES), jnp.float32)
        for r in range(rows):
            acc = acc + test_ref[:, r * LANES : (r + 1) * LANES] * phi[r : r + 1, :]
        weighted.append(acc)
    ones = jnp.ones((8, LANES), jnp.float32)
    sums = nt_dot(ones, jnp.concatenate(weighted, axis=0), precision=HIGHEST) * score_scale
    for x in range(ex_dev):
        scores_ref[x : x + 1, :] = sums[0:1, x * tests : (x + 1) * tests]
    me = lax.axis_index("fsdp")
    own = phi_ref[pl.ds(me // 2, ex_dev, stride=rows), :]
    own = jnp.where(me % 2 == 0, own, pltpu.roll(own, LANES // 2, 1))
    for r in range(rows):
        send_ref[r, :ex_dev, :] = phi_ref[pl.ds(r, ex_dev, stride=rows), :]
        send_ref[r, ex_dev:, :] = own


def tile_kernel(ex_all, recv_ref, out_ref):
    groups, both, _ = recv_ref.shape
    half = both // 2
    recv = recv_ref[...]
    first = lax.broadcasted_iota(jnp.int32, recv.shape, 1) < half
    cols = jnp.where(first, recv, 0.0).reshape(groups * both, LANES)
    swapped = jnp.concatenate([recv[:, half:], recv[:, :half]], axis=1)
    rows = jnp.where(first, swapped, 0.0).reshape(groups * both, LANES)
    tile = lax.dot_general(
        rows, cols, (((0,), (0,)), ((), ())), preferred_element_type=jnp.float32, precision=HIGHEST
    )
    height = out_ref.shape[0]
    row_start = lax.axis_index("fsdp") * height
    col_start = lax.axis_index("ex") * LANES
    row_index = row_start + lax.broadcasted_iota(jnp.int32, out_ref.shape, 0)
    col_index = col_start + lax.broadcasted_iota(jnp.int32, out_ref.shape, 1)
    eye = jnp.where(row_index == col_index, 1.0, 0.0).astype(jnp.float32)
    out_ref[...] = tile[:height] * (1.0 / ex_all) + eye


def shards(activations, out_grads, in_factor, out_factor, test_features):
    fsdp_count = lax.axis_size("fsdp")
    ex_count = lax.axis_size("ex")
    rows_total, in_width = activations.shape
    out_width = out_grads.shape[1]
    in_rank = in_factor.shape[1]
    out_rank = out_factor.shape[1]
    rank = in_rank + out_rank
    features = in_rank * out_rank
    ex_dev = rows_total // LEN
    tests = test_features.shape[0]
    feature_rows = features // LANES
    steps = 4
    block = rows_total // steps
    f32 = jnp.float32

    chunks = pl.pallas_call(
        project_kernel,
        grid=(steps,),
        in_specs=[
            pl.BlockSpec((block, in_width), lambda i: (i, 0)),
            pl.BlockSpec((out_width, block), lambda i: (0, i)),
            pl.BlockSpec((in_rank, in_width), lambda i: (0, 0)),
            pl.BlockSpec((out_rank, out_width), lambda i: (0, 0)),
        ],
        out_specs=pl.BlockSpec((block // LANES, rank, LANES), lambda i: (i, 0, 0)),
        out_shape=jax.ShapeDtypeStruct((fsdp_count, rank, LANES), f32),
        compiler_params=LIMIT,
        name="project",
    )(activations, out_grads.T, in_factor.T, out_factor.T)
    near, far = block_groups(fsdp_count)
    near_parts = lax.all_to_all(chunks, "fsdp", 0, 0, tiled=True, axis_index_groups=near)
    near_sum = pl.pallas_call(
        sum_kernel,
        in_specs=[VMEM],
        out_specs=VMEM,
        out_shape=jax.ShapeDtypeStruct((len(far[0]), rank, LANES), f32),
        compiler_params=LIMIT,
        name="near_sum",
    )(near_parts.reshape(len(near[0]), len(far[0]), rank, LANES))
    parts = lax.all_to_all(near_sum, "fsdp", 0, 0, tiled=True, axis_index_groups=far)

    outer = pl.pallas_call(
        functools.partial(outer_kernel, in_rank),
        in_specs=[VMEM],
        out_specs=VMEM,
        out_shape=jax.ShapeDtypeStruct((fsdp_count, feature_rows, LANES), f32),
        scratch_shapes=[pltpu.VMEM((rank, LANES), f32)],
        compiler_params=LIMIT,
        name="outer",
    )(parts)
    partials = lax.all_to_all(outer, "fsdp", 0, 0, tiled=True)

    send, scores_t = pl.pallas_call(
        functools.partial(scores_kernel, 1.0 / math.sqrt(LEN), 1.0 / math.sqrt(features)),
        in_specs=[VMEM, VMEM],
        out_specs=[VMEM, VMEM],
        out_shape=[
            jax.ShapeDtypeStruct((ex_count, 2 * ex_dev, LANES), f32),
            jax.ShapeDtypeStruct((ex_dev, tests), f32),
        ],
        scratch_shapes=[pltpu.VMEM((ex_dev * feature_rows, LANES), f32)],
        compiler_params=LIMIT,
        name="scores",
    )(partials, test_features)
    recv = lax.all_to_all(send, "ex", 0, 0, tiled=True)

    kernel = pl.pallas_call(
        functools.partial(tile_kernel, ex_dev * ex_count),
        in_specs=[VMEM],
        out_specs=VMEM,
        out_shape=jax.ShapeDtypeStruct((features // fsdp_count, features // ex_count), f32),
        compiler_params=LIMIT,
        name="tile",
    )(recv)
    return (kernel, scores_t.T)


def solution(mesh):
    in_specs = (P("ex", "fsdp"), P("ex", "fsdp"), P("fsdp", None), P("fsdp", None), P("fsdp", None))
    out_specs = (P("fsdp", "ex"), P("fsdp", "ex"))
    return jax.shard_map(shards, mesh=mesh, in_specs=in_specs, out_specs=out_specs, check_vma=False)
```

```python
import functools
import math

import jax
import jax.numpy as jnp
from jax import lax
from jax.experimental import pallas as pl
from jax.experimental.pallas import tpu as pltpu
from jax.sharding import PartitionSpec as P

LEN = 1024
LANES = 128
Z = 4
LIMIT = pltpu.CompilerParams(vmem_limit_bytes=16 * 2**20)
HIGHEST = lax.Precision.HIGHEST
VMEM = pl.BlockSpec(memory_space=pltpu.VMEM)
HBM = pl.BlockSpec(memory_space=pltpu.HBM)


def nt_dot(a, b, **kw):
    return lax.dot_general(a, b, (((1,), (1,)), ((), ())), preferred_element_type=jnp.float32, **kw)


def project_kernel(act_hbm, grad_t_hbm, in_t_hbm, out_t_hbm, chunk_hbm, act, grad_t, in_t, out_t, chunk, sems, out_sems):
    steps, block, _ = act.shape
    in_rank = in_t.shape[0]
    slices = block // LANES
    weights = [
        pltpu.make_async_copy(in_t_hbm, in_t, sems.at[0]),
        pltpu.make_async_copy(out_t_hbm, out_t, sems.at[1]),
    ]
    acts, grads, outs = [], [], []
    for i in range(steps):
        rows = pl.ds(i * block, block)
        own = pl.ds(i * slices, slices)
        acts.append(pltpu.make_async_copy(act_hbm.at[rows, :], act.at[i], sems.at[2 + 2 * i]))
        grads.append(pltpu.make_async_copy(grad_t_hbm.at[:, rows], grad_t.at[i], sems.at[3 + 2 * i]))
        outs.append(pltpu.make_async_copy(chunk.at[own], chunk_hbm.at[own], out_sems.at[i]))
    for copy in weights:
        copy.start()
    for i in range(steps):
        acts[i].start()
        grads[i].start()
    for copy in weights:
        copy.wait()
    for i in range(steps):
        acts[i].wait()
        proj_in = nt_dot(in_t[...], act[i])
        grads[i].wait()
        proj_out = jnp.dot(out_t[...], grad_t[i], preferred_element_type=jnp.float32)
        for s in range(slices):
            cols = slice(s * LANES, (s + 1) * LANES)
            chunk[i * slices + s, :in_rank, :] = proj_in[:, cols]
            chunk[i * slices + s, in_rank:, :] = proj_out[:, cols]
        outs[i].start()
    for copy in outs:
        copy.wait()


def block_groups(fsdp_count):
    blocks = range(fsdp_count // Z // 2)
    place = lambda y, z, dy, dz: (2 * y + dy) * Z + 2 * z + dz
    pair, halves = range(2), range(Z // 2)
    near = [[place(y, z, dy, dz) for dy in pair for dz in pair] for y in blocks for z in halves]
    far = [[place(y, z, dy, dz) for y in blocks for z in halves] for dy in pair for dz in pair]
    return near, far


def sum_kernel(parts_ref, out_ref):
    total = parts_ref[0]
    for s in range(1, parts_ref.shape[0]):
        total = total + parts_ref[s]
    out_ref[...] = total


def outer_kernel(in_rank, parts_ref, out_ref, sum_ref):
    total = parts_ref[0]
    for s in range(1, parts_ref.shape[0]):
        total = total + parts_ref[s]
    sum_ref[...] = total
    out_rank = total.shape[0] - in_rank
    per_row = LANES // out_rank
    rows = in_rank // per_row
    proj_in = jnp.concatenate(
        [sum_ref[pl.ds(a, rows, stride=per_row), :] for a in range(per_row)], axis=0
    )
    proj_out = jnp.concatenate([total[in_rank:]] * per_row, axis=0)
    full = nt_dot(proj_in, proj_out, precision=HIGHEST)
    group = lax.broadcasted_iota(jnp.int32, (rows, LANES), 1) // out_rank
    dense = full[:rows]
    for a in range(1, per_row):
        dense = jnp.where(group == a, full[a * rows : (a + 1) * rows], dense)
    out_ref[...] = jnp.broadcast_to(dense[None], out_ref.shape)


def scores_kernel(factor_scale, score_scale, parts_ref, test_ref, send_ref, scores_ref, phi_ref):
    sources, rows, _ = parts_ref.shape
    ex_dev = scores_ref.shape[0]
    near = lambda f: f // Z % 2 * 2 + f % 2
    tests = test_ref.shape[0]
    weighted = []
    for x in range(ex_dev):
        phi = sum(parts_ref[f] for f in range(sources) if near(f) == x) * factor_scale
        phi_ref[x * rows : (x + 1) * rows, :] = phi
        acc = jnp.zeros((tests, LANES), jnp.float32)
        for r in range(rows):
            acc = acc + test_ref[:, r * LANES : (r + 1) * LANES] * phi[r : r + 1, :]
        weighted.append(acc)
    ones = jnp.ones((8, LANES), jnp.float32)
    sums = nt_dot(ones, jnp.concatenate(weighted, axis=0), precision=HIGHEST) * score_scale
    for x in range(ex_dev):
        scores_ref[x : x + 1, :] = sums[0:1, x * tests : (x + 1) * tests]
    me = lax.axis_index("fsdp")
    own = phi_ref[pl.ds(me // 2, ex_dev, stride=rows), :]
    own = jnp.where(me % 2 == 0, own, pltpu.roll(own, LANES // 2, 1))
    for r in range(rows):
        send_ref[r, :ex_dev, :] = phi_ref[pl.ds(r, ex_dev, stride=rows), :]
        send_ref[r, ex_dev:, :] = own


def tile_kernel(ex_all, recv_ref, out_ref):
    groups, both, _ = recv_ref.shape
    half = both // 2
    recv = recv_ref[...]
    first = lax.broadcasted_iota(jnp.int32, recv.shape, 1) < half
    cols = jnp.where(first, recv, 0.0).reshape(groups * both, LANES)
    swapped = jnp.concatenate([recv[:, half:], recv[:, :half]], axis=1)
    rows = jnp.where(first, swapped, 0.0).reshape(groups * both, LANES)
    tile = lax.dot_general(
        rows, cols, (((0,), (0,)), ((), ())), preferred_element_type=jnp.float32, precision=HIGHEST
    )
    height = out_ref.shape[0]
    row_start = lax.axis_index("fsdp") * height
    col_start = lax.axis_index("ex") * LANES
    row_index = row_start + lax.broadcasted_iota(jnp.int32, out_ref.shape, 0)
    col_index = col_start + lax.broadcasted_iota(jnp.int32, out_ref.shape, 1)
    eye = jnp.where(row_index == col_index, 1.0, 0.0).astype(jnp.float32)
    out_ref[...] = tile[:height] * (1.0 / ex_all) + eye


def shards(activations, out_grads, in_factor, out_factor, test_features):
    fsdp_count = lax.axis_size("fsdp")
    ex_count = lax.axis_size("ex")
    rows_total, in_width = activations.shape
    out_width = out_grads.shape[1]
    in_rank = in_factor.shape[1]
    out_rank = out_factor.shape[1]
    rank = in_rank + out_rank
    features = in_rank * out_rank
    ex_dev = rows_total // LEN
    tests = test_features.shape[0]
    feature_rows = features // LANES
    steps = 2
    block = rows_total // steps
    f32 = jnp.float32

    bf16 = activations.dtype
    chunks = pl.pallas_call(
        project_kernel,
        in_specs=[HBM] * 4,
        out_specs=HBM,
        out_shape=jax.ShapeDtypeStruct((fsdp_count, rank, LANES), f32),
        scratch_shapes=[
            pltpu.VMEM((steps, block, in_width), bf16),
            pltpu.VMEM((steps, out_width, block), bf16),
            pltpu.VMEM((in_rank, in_width), bf16),
            pltpu.VMEM((out_rank, out_width), bf16),
            pltpu.VMEM((fsdp_count, rank, LANES), f32),
            pltpu.SemaphoreType.DMA((2 + 2 * steps,)),
            pltpu.SemaphoreType.DMA((steps,)),
        ],
        compiler_params=pltpu.CompilerParams(vmem_limit_bytes=58 * 2**20),
        name="project",
    )(activations, out_grads.T, in_factor.T, out_factor.T)
    near, far = block_groups(fsdp_count)
    near_parts = lax.all_to_all(chunks, "fsdp", 0, 0, tiled=True, axis_index_groups=near)
    near_sum = pl.pallas_call(
        sum_kernel,
        in_specs=[VMEM],
        out_specs=VMEM,
        out_shape=jax.ShapeDtypeStruct((len(far[0]), rank, LANES), f32),
        compiler_params=LIMIT,
        name="near_sum",
    )(near_parts.reshape(len(near[0]), len(far[0]), rank, LANES))
    parts = lax.all_to_all(near_sum, "fsdp", 0, 0, tiled=True, axis_index_groups=far)

    outer = pl.pallas_call(
        functools.partial(outer_kernel, in_rank),
        in_specs=[VMEM],
        out_specs=VMEM,
        out_shape=jax.ShapeDtypeStruct((fsdp_count, feature_rows, LANES), f32),
        scratch_shapes=[pltpu.VMEM((rank, LANES), f32)],
        compiler_params=LIMIT,
        name="outer",
    )(parts)
    partials = lax.all_to_all(outer, "fsdp", 0, 0, tiled=True)

    send, scores_t = pl.pallas_call(
        functools.partial(scores_kernel, 1.0 / math.sqrt(LEN), 1.0 / math.sqrt(features)),
        in_specs=[VMEM, VMEM],
        out_specs=[VMEM, VMEM],
        out_shape=[
            jax.ShapeDtypeStruct((ex_count, 2 * ex_dev, LANES), f32),
            jax.ShapeDtypeStruct((ex_dev, tests), f32),
        ],
        scratch_shapes=[pltpu.VMEM((ex_dev * feature_rows, LANES), f32)],
        compiler_params=LIMIT,
        name="scores",
    )(partials, test_features)
    recv = lax.all_to_all(send, "ex", 0, 0, tiled=True)

    kernel = pl.pallas_call(
        functools.partial(tile_kernel, ex_dev * ex_count),
        in_specs=[VMEM],
        out_specs=VMEM,
        out_shape=jax.ShapeDtypeStruct((features // fsdp_count, features // ex_count), f32),
        compiler_params=LIMIT,
        name="tile",
    )(recv)
    return (kernel, scores_t.T)


def solution(mesh):
    in_specs = (P("ex", "fsdp"), P("ex", "fsdp"), P("fsdp", None), P("fsdp", None), P("fsdp", None))
    out_specs = (P("fsdp", "ex"), P("fsdp", "ex"))
    return jax.shard_map(shards, mesh=mesh, in_specs=in_specs, out_specs=out_specs, check_vma=False)
```

```python
import functools
import math

import jax
import jax.numpy as jnp
from jax import lax
from jax.experimental import pallas as pl
from jax.experimental.pallas import tpu as pltpu
from jax.sharding import PartitionSpec as P

LEN = 1024
LANES = 128
Z = 4
LIMIT = pltpu.CompilerParams(vmem_limit_bytes=16 * 2**20)
HIGHEST = lax.Precision.HIGHEST
VMEM = pl.BlockSpec(memory_space=pltpu.VMEM)


def nt_dot(a, b, **kw):
    return lax.dot_general(a, b, (((1,), (1,)), ((), ())), preferred_element_type=jnp.float32, **kw)


def block_place(f):
    return f // Z % 2 * 2 + f % 2


def place_order(ex_count):
    own = block_place(lax.axis_index("fsdp"))
    first = 2 - lax.axis_index("ex") % 2
    return own ^ first, own ^ 3, own, own ^ 3 ^ first


def project_kernel(along_rows, ex_count, arg_ref, weights_ref, give_ref, keep_ref):
    for k, place in enumerate(place_order(ex_count)):
        own = pl.ds(pl.multiple_of(place * LEN, LEN), LEN)
        if along_rows:
            proj = nt_dot(weights_ref[...], arg_ref[own, :])
        else:
            proj = jnp.dot(weights_ref[...], arg_ref[:, own], preferred_element_type=jnp.float32)
        out_ref = keep_ref if k >= 2 else give_ref
        for s in range(LEN // LANES):
            out_ref[k % 2, s] = proj[:, s * LANES : (s + 1) * LANES]


def block_groups(fsdp_count):
    blocks = range(fsdp_count // Z // 2)
    place = lambda y, z, dy, dz: (2 * y + dy) * Z + 2 * z + dz
    pair, halves = range(2), range(Z // 2)
    near = [[place(y, z, dy, dz) for dy in pair for dz in pair] for y in blocks for z in halves]
    far = [[place(y, z, dy, dz) for y in blocks for z in halves] for dy in pair for dz in pair]
    return near, far


def pair_sum_kernel(keep_ref, recv_ref, keep_next_ref, give_next_ref):
    keep_next_ref[...] = keep_ref[0] + recv_ref[0]
    give_next_ref[...] = keep_ref[1] + recv_ref[1]


def near_sum_kernel(keep_in_ref, recv_in_ref, keep_out_ref, recv_out_ref, sum_ref):
    in_rank = keep_in_ref.shape[1]
    sum_ref[:, :in_rank, :] = keep_in_ref[...] + recv_in_ref[...]
    sum_ref[:, in_rank:, :] = keep_out_ref[...] + recv_out_ref[...]


def outer_kernel(in_rank, parts_ref, out_ref, sum_ref):
    total = parts_ref[0]
    for s in range(1, parts_ref.shape[0]):
        total = total + parts_ref[s]
    sum_ref[...] = total
    out_rank = total.shape[0] - in_rank
    per_row = LANES // out_rank
    rows = in_rank // per_row
    proj_in = jnp.concatenate(
        [sum_ref[pl.ds(a, rows, stride=per_row), :] for a in range(per_row)], axis=0
    )
    proj_out = jnp.concatenate([total[in_rank:]] * per_row, axis=0)
    full = nt_dot(proj_in, proj_out, precision=HIGHEST)
    group = lax.broadcasted_iota(jnp.int32, (rows, LANES), 1) // out_rank
    dense = full[:rows]
    for a in range(1, per_row):
        dense = jnp.where(group == a, full[a * rows : (a + 1) * rows], dense)
    out_ref[...] = jnp.broadcast_to(dense[None], out_ref.shape)


def features_kernel(factor_scale, ex_dev, parts_ref, phi_ref, send_ref):
    sources, rows, _ = parts_ref.shape
    for x in range(ex_dev):
        phi = sum(parts_ref[f] for f in range(sources) if block_place(f) == x) * factor_scale
        phi_ref[x * rows : (x + 1) * rows, :] = phi
    me = lax.axis_index("fsdp")
    own = phi_ref[pl.ds(me // 2, ex_dev, stride=rows), :]
    own = jnp.where(me % 2 == 0, own, pltpu.roll(own, LANES // 2, 1))
    for r in range(rows):
        send_ref[r, :ex_dev, :] = phi_ref[pl.ds(r, ex_dev, stride=rows), :]
        send_ref[r, ex_dev:, :] = own


def scores_kernel(score_scale, phi_ref, test_ref, scores_ref):
    ex_dev, tests = scores_ref.shape
    rows = phi_ref.shape[0] // ex_dev
    weighted = []
    for x in range(ex_dev):
        phi = phi_ref[x * rows : (x + 1) * rows, :]
        acc = jnp.zeros((tests, LANES), jnp.float32)
        for r in range(rows):
            acc = acc + test_ref[:, r * LANES : (r + 1) * LANES] * phi[r : r + 1, :]
        weighted.append(acc)
    ones = jnp.ones((8, LANES), jnp.float32)
    sums = nt_dot(ones, jnp.concatenate(weighted, axis=0), precision=HIGHEST) * score_scale
    for x in range(ex_dev):
        scores_ref[x : x + 1, :] = sums[0:1, x * tests : (x + 1) * tests]


def tile_kernel(ex_all, recv_ref, out_ref):
    groups, both, _ = recv_ref.shape
    half = both // 2
    recv = recv_ref[...]
    first = lax.broadcasted_iota(jnp.int32, recv.shape, 1) < half
    cols = jnp.where(first, recv, 0.0).reshape(groups * both, LANES)
    swapped = jnp.concatenate([recv[:, half:], recv[:, :half]], axis=1)
    rows = jnp.where(first, swapped, 0.0).reshape(groups * both, LANES)
    tile = lax.dot_general(
        rows, cols, (((0,), (0,)), ((), ())), preferred_element_type=jnp.float32, precision=HIGHEST
    )
    height = out_ref.shape[0]
    row_start = lax.axis_index("fsdp") * height
    col_start = lax.axis_index("ex") * LANES
    row_index = row_start + lax.broadcasted_iota(jnp.int32, out_ref.shape, 0)
    col_index = col_start + lax.broadcasted_iota(jnp.int32, out_ref.shape, 1)
    eye = jnp.where(row_index == col_index, 1.0, 0.0).astype(jnp.float32)
    out_ref[...] = tile[:height] * (1.0 / ex_all) + eye


def shards(activations, out_grads, in_factor, out_factor, test_features):
    fsdp_count = lax.axis_size("fsdp")
    ex_count = lax.axis_size("ex")
    rows_total, in_width = activations.shape
    out_width = out_grads.shape[1]
    in_rank = in_factor.shape[1]
    out_rank = out_factor.shape[1]
    rank = in_rank + out_rank
    features = in_rank * out_rank
    ex_dev = rows_total // LEN
    tests = test_features.shape[0]
    feature_rows = features // LANES
    f32 = jnp.float32
    near, far = block_groups(fsdp_count)
    slices = len(far[0])

    def swap(value, step):
        pairs = []
        for e in range(ex_count):
            mask = 2 - e % 2 if step == 0 else 1 + e % 2
            for group in near:
                pairs += [(f * ex_count + e, group[b ^ mask] * ex_count + e) for b, f in enumerate(group)]
        return lax.ppermute(value, ("fsdp", "ex"), pairs)

    def project(arg, weights, along_rows, name):
        out_shape = jax.ShapeDtypeStruct((2, slices, weights.shape[0], LANES), f32)
        return pl.pallas_call(
            functools.partial(project_kernel, along_rows, ex_count),
            in_specs=[VMEM] * 2,
            out_specs=[VMEM] * 2,
            out_shape=[out_shape] * 2,
            compiler_params=LIMIT,
            name=name,
        )(arg, weights)

    def pair_sum(keep, recv):
        out_shape = jax.ShapeDtypeStruct(keep.shape[1:], f32)
        return pl.pallas_call(
            pair_sum_kernel,
            in_specs=[VMEM] * 2,
            out_specs=[VMEM] * 2,
            out_shape=[out_shape] * 2,
            compiler_params=LIMIT,
            name="pair_sum",
        )(keep, recv)

    give_in, keep_in = project(activations, in_factor.T, True, "project_in")
    give_in, keep_in, out_grads = lax.optimization_barrier((give_in, keep_in, out_grads))
    recv_in = swap(give_in, 0)
    give_out, keep_out = project(out_grads.T, out_factor.T, False, "project_out")
    recv_out = swap(give_out, 0)
    keep_in, give_in = pair_sum(keep_in, recv_in)
    recv_in = swap(give_in, 1)
    keep_out, give_out = pair_sum(keep_out, recv_out)
    recv_out = swap(give_out, 1)
    near_sum = pl.pallas_call(
        near_sum_kernel,
        in_specs=[VMEM] * 4,
        out_specs=VMEM,
        out_shape=jax.ShapeDtypeStruct((slices, rank, LANES), f32),
        compiler_params=LIMIT,
        name="near_sum",
    )(keep_in, recv_in, keep_out, recv_out)
    parts = lax.all_to_all(near_sum, "fsdp", 0, 0, tiled=True, axis_index_groups=far)

    outer = pl.pallas_call(
        functools.partial(outer_kernel, in_rank),
        in_specs=[VMEM],
        out_specs=VMEM,
        out_shape=jax.ShapeDtypeStruct((fsdp_count, feature_rows, LANES), f32),
        scratch_shapes=[pltpu.VMEM((rank, LANES), f32)],
        compiler_params=LIMIT,
        name="outer",
    )(parts)
    partials = lax.all_to_all(outer, "fsdp", 0, 0, tiled=True)

    phi, send = pl.pallas_call(
        functools.partial(features_kernel, 1.0 / math.sqrt(LEN), ex_dev),
        in_specs=[VMEM],
        out_specs=[VMEM, VMEM],
        out_shape=[
            jax.ShapeDtypeStruct((ex_dev * feature_rows, LANES), f32),
            jax.ShapeDtypeStruct((ex_count, 2 * ex_dev, LANES), f32),
        ],
        compiler_params=LIMIT,
        name="features",
    )(partials)
    recv = lax.all_to_all(send, "ex", 0, 0, tiled=True)
    scores_t = pl.pallas_call(
        functools.partial(scores_kernel, 1.0 / math.sqrt(features)),
        in_specs=[VMEM, VMEM],
        out_specs=VMEM,
        out_shape=jax.ShapeDtypeStruct((ex_dev, tests), f32),
        compiler_params=LIMIT,
        name="scores",
    )(phi, test_features)

    kernel = pl.pallas_call(
        functools.partial(tile_kernel, ex_dev * ex_count),
        in_specs=[VMEM],
        out_specs=VMEM,
        out_shape=jax.ShapeDtypeStruct((features // fsdp_count, features // ex_count), f32),
        compiler_params=LIMIT,
        name="tile",
    )(recv)
    return (kernel, scores_t.T)


def solution(mesh):
    in_specs = (P("ex", "fsdp"), P("ex", "fsdp"), P("fsdp", None), P("fsdp", None), P("fsdp", None))
    out_specs = (P("fsdp", "ex"), P("fsdp", "ex"))
    return jax.shard_map(shards, mesh=mesh, in_specs=in_specs, out_specs=out_specs, check_vma=False)
```

```python
import functools
import math

import jax
import jax.numpy as jnp
from jax import lax
from jax.experimental import pallas as pl
from jax.experimental.pallas import tpu as pltpu
from jax.sharding import PartitionSpec as P

LEN = 1024
LANES = 128
Z = 4
LIMIT = pltpu.CompilerParams(vmem_limit_bytes=16 * 2**20)
HIGHEST = lax.Precision.HIGHEST
VMEM = pl.BlockSpec(memory_space=pltpu.VMEM)


def nt_dot(a, b, **kw):
    return lax.dot_general(a, b, (((1,), (1,)), ((), ())), preferred_element_type=jnp.float32, **kw)


def block_place(f):
    return f // Z % 2 * 2 + f % 2


def place_order(ex_count):
    own = block_place(lax.axis_index("fsdp"))
    first = 2 - lax.axis_index("ex") % 2
    return own ^ first, own ^ 3, own, own ^ 3 ^ first


def project_kernel(along_rows, ex_count, arg_ref, weights_ref, give_ref, keep_ref):
    for k, place in enumerate(place_order(ex_count)):
        own = pl.ds(pl.multiple_of(place * LEN, LEN), LEN)
        if along_rows:
            proj = nt_dot(weights_ref[...], arg_ref[own, :])
        else:
            proj = jnp.dot(weights_ref[...], arg_ref[:, own], preferred_element_type=jnp.float32)
        out_ref = keep_ref if k >= 2 else give_ref
        for s in range(LEN // LANES):
            out_ref[k % 2, s] = proj[:, s * LANES : (s + 1) * LANES]


def block_groups(fsdp_count):
    blocks = range(fsdp_count // Z // 2)
    place = lambda y, z, dy, dz: (2 * y + dy) * Z + 2 * z + dz
    pair, halves = range(2), range(Z // 2)
    near = [[place(y, z, dy, dz) for dy in pair for dz in pair] for y in blocks for z in halves]
    far = [[place(y, z, dy, dz) for y in blocks for z in halves] for dy in pair for dz in pair]
    return near, far


def pair_sum_kernel(keep_ref, recv_ref, keep_next_ref, give_next_ref):
    keep_next_ref[...] = keep_ref[0] + recv_ref[0]
    give_next_ref[...] = keep_ref[1] + recv_ref[1]


def near_sum_kernel(keep_in_ref, recv_in_ref, keep_out_ref, recv_out_ref, sum_ref):
    in_rank = keep_in_ref.shape[1]
    sum_ref[:, :in_rank, :] = keep_in_ref[...] + recv_in_ref[...]
    sum_ref[:, in_rank:, :] = keep_out_ref[...] + recv_out_ref[...]


def outer_kernel(in_rank, parts_ref, out_ref, sum_ref):
    total = parts_ref[0]
    for s in range(1, parts_ref.shape[0]):
        total = total + parts_ref[s]
    sum_ref[...] = total
    out_rank = total.shape[0] - in_rank
    per_row = LANES // out_rank
    rows = in_rank // per_row
    proj_in = jnp.concatenate(
        [sum_ref[pl.ds(a, rows, stride=per_row), :] for a in range(per_row)], axis=0
    )
    proj_out = jnp.concatenate([total[in_rank:]] * per_row, axis=0)
    full = nt_dot(proj_in, proj_out, precision=HIGHEST)
    group = lax.broadcasted_iota(jnp.int32, (rows, LANES), 1) // out_rank
    dense = full[:rows]
    for a in range(1, per_row):
        dense = jnp.where(group == a, full[a * rows : (a + 1) * rows], dense)
    out_ref[...] = jnp.broadcast_to(dense[None], out_ref.shape)


def features_kernel(factor_scale, score_scale, parts_ref, test_ref, send_ref, scores_ref, phi_ref):
    sources, rows, _ = parts_ref.shape
    ex_dev, tests = scores_ref.shape
    weighted = []
    for x in range(ex_dev):
        phi = sum(parts_ref[f] for f in range(sources) if block_place(f) == x) * factor_scale
        phi_ref[x * rows : (x + 1) * rows, :] = phi
        acc = jnp.zeros((tests, LANES), jnp.float32)
        for r in range(rows):
            acc = acc + test_ref[:, r * LANES : (r + 1) * LANES] * phi[r : r + 1, :]
        weighted.append(acc)
    me = lax.axis_index("fsdp")
    own = phi_ref[pl.ds(me // 2, ex_dev, stride=rows), :]
    own = jnp.where(me % 2 == 0, own, pltpu.roll(own, LANES // 2, 1))
    for r in range(rows):
        send_ref[r, :ex_dev, :] = phi_ref[pl.ds(r, ex_dev, stride=rows), :]
        send_ref[r, ex_dev:, :] = own
    ones = jnp.ones((8, LANES), jnp.float32)
    sums = nt_dot(ones, jnp.concatenate(weighted, axis=0), precision=HIGHEST) * score_scale
    for x in range(ex_dev):
        scores_ref[x : x + 1, :] = sums[0:1, x * tests : (x + 1) * tests]


def tile_kernel(ex_all, recv_ref, scores_ref, out_ref, scores_out_ref):
    scores_out_ref[...] = scores_ref[...]
    groups, both, _ = recv_ref.shape
    half = both // 2
    recv = recv_ref[...]
    first = lax.broadcasted_iota(jnp.int32, recv.shape, 1) < half
    cols = jnp.where(first, recv, 0.0).reshape(groups * both, LANES)
    swapped = jnp.concatenate([recv[:, half:], recv[:, :half]], axis=1)
    rows = jnp.where(first, swapped, 0.0).reshape(groups * both, LANES)
    tile = lax.dot_general(
        rows, cols, (((0,), (0,)), ((), ())), preferred_element_type=jnp.float32, precision=HIGHEST
    )
    height = out_ref.shape[0]
    row_start = lax.axis_index("fsdp") * height
    col_start = lax.axis_index("ex") * LANES
    row_index = row_start + lax.broadcasted_iota(jnp.int32, out_ref.shape, 0)
    col_index = col_start + lax.broadcasted_iota(jnp.int32, out_ref.shape, 1)
    eye = jnp.where(row_index == col_index, 1.0, 0.0).astype(jnp.float32)
    out_ref[...] = tile[:height] * (1.0 / ex_all) + eye


def shards(activations, out_grads, in_factor, out_factor, test_features):
    fsdp_count = lax.axis_size("fsdp")
    ex_count = lax.axis_size("ex")
    rows_total, in_width = activations.shape
    out_width = out_grads.shape[1]
    in_rank = in_factor.shape[1]
    out_rank = out_factor.shape[1]
    rank = in_rank + out_rank
    features = in_rank * out_rank
    ex_dev = rows_total // LEN
    tests = test_features.shape[0]
    feature_rows = features // LANES
    f32 = jnp.float32
    near, far = block_groups(fsdp_count)
    slices = len(far[0])

    def swap(value, step):
        pairs = []
        for e in range(ex_count):
            mask = 2 - e % 2 if step == 0 else 1 + e % 2
            for group in near:
                pairs += [(f * ex_count + e, group[b ^ mask] * ex_count + e) for b, f in enumerate(group)]
        return lax.ppermute(value, ("fsdp", "ex"), pairs)

    def project(arg, weights, along_rows, name):
        out_shape = jax.ShapeDtypeStruct((2, slices, weights.shape[0], LANES), f32)
        return pl.pallas_call(
            functools.partial(project_kernel, along_rows, ex_count),
            in_specs=[VMEM] * 2,
            out_specs=[VMEM] * 2,
            out_shape=[out_shape] * 2,
            compiler_params=LIMIT,
            name=name,
        )(arg, weights)

    def pair_sum(keep, recv):
        out_shape = jax.ShapeDtypeStruct(keep.shape[1:], f32)
        return pl.pallas_call(
            pair_sum_kernel,
            in_specs=[VMEM] * 2,
            out_specs=[VMEM] * 2,
            out_shape=[out_shape] * 2,
            compiler_params=LIMIT,
            name="pair_sum",
        )(keep, recv)

    give_in, keep_in = project(activations, in_factor.T, True, "project_in")
    give_in, keep_in, out_grads = lax.optimization_barrier((give_in, keep_in, out_grads))
    recv_in = swap(give_in, 0)
    give_out, keep_out = project(out_grads.T, out_factor.T, False, "project_out")
    recv_out = swap(give_out, 0)
    keep_in, give_in = pair_sum(keep_in, recv_in)
    recv_in = swap(give_in, 1)
    keep_out, give_out = pair_sum(keep_out, recv_out)
    recv_out = swap(give_out, 1)
    near_sum = pl.pallas_call(
        near_sum_kernel,
        in_specs=[VMEM] * 4,
        out_specs=VMEM,
        out_shape=jax.ShapeDtypeStruct((slices, rank, LANES), f32),
        compiler_params=LIMIT,
        name="near_sum",
    )(keep_in, recv_in, keep_out, recv_out)
    parts = lax.all_to_all(near_sum, "fsdp", 0, 0, tiled=True, axis_index_groups=far)

    outer = pl.pallas_call(
        functools.partial(outer_kernel, in_rank),
        in_specs=[VMEM],
        out_specs=VMEM,
        out_shape=jax.ShapeDtypeStruct((fsdp_count, feature_rows, LANES), f32),
        scratch_shapes=[pltpu.VMEM((rank, LANES), f32)],
        compiler_params=LIMIT,
        name="outer",
    )(parts)
    partials = lax.all_to_all(outer, "fsdp", 0, 0, tiled=True)

    scores_shape = jax.ShapeDtypeStruct((ex_dev, tests), f32)
    send, scores = pl.pallas_call(
        functools.partial(features_kernel, 1.0 / math.sqrt(LEN), 1.0 / math.sqrt(features)),
        in_specs=[VMEM, VMEM],
        out_specs=[VMEM, VMEM],
        out_shape=[jax.ShapeDtypeStruct((ex_count, 2 * ex_dev, LANES), f32), scores_shape],
        scratch_shapes=[pltpu.VMEM((ex_dev * feature_rows, LANES), f32)],
        compiler_params=LIMIT,
        name="features",
    )(partials, test_features)
    recv = lax.all_to_all(send, "ex", 0, 0, tiled=True)
    kernel, scores_t = pl.pallas_call(
        functools.partial(tile_kernel, ex_dev * ex_count),
        in_specs=[VMEM, VMEM],
        out_specs=[VMEM, VMEM],
        out_shape=[
            jax.ShapeDtypeStruct((features // fsdp_count, features // ex_count), f32),
            scores_shape,
        ],
        compiler_params=LIMIT,
        name="tile",
    )(recv, scores)
    return (kernel, scores_t.T)


def solution(mesh):
    in_specs = (P("ex", "fsdp"), P("ex", "fsdp"), P("fsdp", None), P("fsdp", None), P("fsdp", None))
    out_specs = (P("fsdp", "ex"), P("fsdp", "ex"))
    return jax.shard_map(shards, mesh=mesh, in_specs=in_specs, out_specs=out_specs, check_vma=False)
```

```python
import functools
import math

import jax
import jax.numpy as jnp
from jax import lax
from jax.experimental import pallas as pl
from jax.experimental.pallas import tpu as pltpu
from jax.sharding import PartitionSpec as P

LEN = 1024
LANES = 128
EX_ORDER = [10, 5, 12, 9, 14, 3, 0, 8, 13, 2, 15, 6, 11, 1, 4, 7]
GATHER_ORDER = [9, 24, 14, 10, 28, 1, 5, 3, 22, 21, 13, 12, 23, 16, 27, 6, 7, 29, 8, 25, 0, 26, 2, 30, 20, 31, 19, 11, 4, 17, 18, 15]
Z = 4
LIMIT = pltpu.CompilerParams(vmem_limit_bytes=16 * 2**20)
HIGHEST = lax.Precision.HIGHEST
VMEM = pl.BlockSpec(memory_space=pltpu.VMEM)


def nt_dot(a, b, **kw):
    return lax.dot_general(a, b, (((1,), (1,)), ((), ())), preferred_element_type=jnp.float32, **kw)


def block_place(f):
    return f // Z % 2 * 2 + f % 2


def place_order(ex_count):
    own = block_place(lax.axis_index("fsdp"))
    first = 2 - lax.axis_index("ex") % 2
    return own ^ first, own ^ 3, own, own ^ 3 ^ first


def project_kernel(along_rows, ex_count, arg_ref, weights_ref, give_ref, keep_ref):
    for k, place in enumerate(place_order(ex_count)):
        own = pl.ds(pl.multiple_of(place * LEN, LEN), LEN)
        if along_rows:
            proj = nt_dot(weights_ref[...], arg_ref[own, :])
        else:
            proj = jnp.dot(weights_ref[...], arg_ref[:, own], preferred_element_type=jnp.float32)
        out_ref = keep_ref if k >= 2 else give_ref
        for s in range(LEN // LANES):
            out_ref[k % 2, s] = proj[:, s * LANES : (s + 1) * LANES]


def block_groups(fsdp_count):
    blocks = range(fsdp_count // Z // 2)
    place = lambda y, z, dy, dz: (2 * y + dy) * Z + 2 * z + dz
    pair, halves = range(2), range(Z // 2)
    near = [[place(y, z, dy, dz) for dy in pair for dz in pair] for y in blocks for z in halves]
    far = [[place(y, z, dy, dz) for y in blocks for z in halves] for dy in pair for dz in pair]
    return near, far


def pair_sum_kernel(keep_ref, recv_ref, keep_next_ref, give_next_ref):
    keep_next_ref[...] = keep_ref[0] + recv_ref[0]
    give_next_ref[...] = keep_ref[1] + recv_ref[1]


def near_sum_kernel(keep_in_ref, recv_in_ref, keep_out_ref, recv_out_ref, sum_ref):
    in_rank = keep_in_ref.shape[1]
    sum_ref[:, :in_rank, :] = keep_in_ref[...] + recv_in_ref[...]
    sum_ref[:, in_rank:, :] = keep_out_ref[...] + recv_out_ref[...]


def outer_kernel(in_rank, parts_ref, out_ref, sum_ref):
    total = parts_ref[0]
    for s in range(1, parts_ref.shape[0]):
        total = total + parts_ref[s]
    sum_ref[...] = total
    out_rank = total.shape[0] - in_rank
    per_row = LANES // out_rank
    rows = in_rank // per_row
    proj_in = jnp.concatenate(
        [sum_ref[pl.ds(a, rows, stride=per_row), :] for a in range(per_row)], axis=0
    )
    proj_out = jnp.concatenate([total[in_rank:]] * per_row, axis=0)
    full = nt_dot(proj_in, proj_out, precision=HIGHEST)
    group = lax.broadcasted_iota(jnp.int32, (rows, LANES), 1) // out_rank
    dense = full[:rows]
    for a in range(1, per_row):
        dense = jnp.where(group == a, full[a * rows : (a + 1) * rows], dense)
    out_ref[...] = jnp.broadcast_to(dense[None], out_ref.shape)


def features_kernel(factor_scale, score_scale, parts_ref, test_ref, send_ref, scores_ref, phi_ref):
    sources, rows, _ = parts_ref.shape
    ex_dev, tests = scores_ref.shape
    weighted = []
    for x in range(ex_dev):
        phi = sum(parts_ref[f] for f in range(sources) if block_place(GATHER_ORDER[f]) == x) * factor_scale
        phi_ref[x * rows : (x + 1) * rows, :] = phi
        acc = jnp.zeros((tests, LANES), jnp.float32)
        for r in range(rows):
            acc = acc + test_ref[:, r * LANES : (r + 1) * LANES] * phi[r : r + 1, :]
        weighted.append(acc)
    me = lax.axis_index("fsdp")
    own = phi_ref[pl.ds(me // 2, ex_dev, stride=rows), :]
    own = jnp.where(me % 2 == 0, own, pltpu.roll(own, LANES // 2, 1))
    for k, r in enumerate(EX_ORDER):
        send_ref[k, :ex_dev, :] = phi_ref[pl.ds(r, ex_dev, stride=rows), :]
        send_ref[k, ex_dev:, :] = own
    ones = jnp.ones((8, LANES), jnp.float32)
    sums = nt_dot(ones, jnp.concatenate(weighted, axis=0), precision=HIGHEST) * score_scale
    for x in range(ex_dev):
        scores_ref[x : x + 1, :] = sums[0:1, x * tests : (x + 1) * tests]


def tile_kernel(ex_all, recv_ref, scores_ref, out_ref, scores_out_ref):
    scores_out_ref[...] = scores_ref[...]
    groups, both, _ = recv_ref.shape
    half = both // 2
    recv = recv_ref[...]
    first = lax.broadcasted_iota(jnp.int32, recv.shape, 1) < half
    cols = jnp.where(first, recv, 0.0).reshape(groups * both, LANES)
    swapped = jnp.concatenate([recv[:, half:], recv[:, :half]], axis=1)
    rows = jnp.where(first, swapped, 0.0).reshape(groups * both, LANES)
    tile = lax.dot_general(
        rows, cols, (((0,), (0,)), ((), ())), preferred_element_type=jnp.float32, precision=HIGHEST
    )
    height = out_ref.shape[0]
    row_start = lax.axis_index("fsdp") * height
    col_start = lax.axis_index("ex") * LANES
    row_index = row_start + lax.broadcasted_iota(jnp.int32, out_ref.shape, 0)
    col_index = col_start + lax.broadcasted_iota(jnp.int32, out_ref.shape, 1)
    eye = jnp.where(row_index == col_index, 1.0, 0.0).astype(jnp.float32)
    out_ref[...] = tile[:height] * (1.0 / ex_all) + eye


def shards(activations, out_grads, in_factor, out_factor, test_features):
    fsdp_count = lax.axis_size("fsdp")
    ex_count = lax.axis_size("ex")
    rows_total, in_width = activations.shape
    out_width = out_grads.shape[1]
    in_rank = in_factor.shape[1]
    out_rank = out_factor.shape[1]
    rank = in_rank + out_rank
    features = in_rank * out_rank
    ex_dev = rows_total // LEN
    tests = test_features.shape[0]
    feature_rows = features // LANES
    f32 = jnp.float32
    near, far = block_groups(fsdp_count)
    slices = len(far[0])

    def swap(value, step):
        pairs = []
        for e in range(ex_count):
            mask = 2 - e % 2 if step == 0 else 1 + e % 2
            for group in near:
                pairs += [(f * ex_count + e, group[b ^ mask] * ex_count + e) for b, f in enumerate(group)]
        return lax.ppermute(value, ("fsdp", "ex"), pairs)

    def project(arg, weights, along_rows, name):
        out_shape = jax.ShapeDtypeStruct((2, slices, weights.shape[0], LANES), f32)
        return pl.pallas_call(
            functools.partial(project_kernel, along_rows, ex_count),
            in_specs=[VMEM] * 2,
            out_specs=[VMEM] * 2,
            out_shape=[out_shape] * 2,
            compiler_params=LIMIT,
            name=name,
        )(arg, weights)

    def pair_sum(keep, recv):
        out_shape = jax.ShapeDtypeStruct(keep.shape[1:], f32)
        return pl.pallas_call(
            pair_sum_kernel,
            in_specs=[VMEM] * 2,
            out_specs=[VMEM] * 2,
            out_shape=[out_shape] * 2,
            compiler_params=LIMIT,
            name="pair_sum",
        )(keep, recv)

    give_in, keep_in = project(activations, in_factor.T, True, "project_in")
    give_in, keep_in, out_grads = lax.optimization_barrier((give_in, keep_in, out_grads))
    recv_in = swap(give_in, 0)
    give_out, keep_out = project(out_grads.T, out_factor.T, False, "project_out")
    recv_out = swap(give_out, 0)
    keep_in, give_in = pair_sum(keep_in, recv_in)
    recv_in = swap(give_in, 1)
    keep_out, give_out = pair_sum(keep_out, recv_out)
    recv_out = swap(give_out, 1)
    near_sum = pl.pallas_call(
        near_sum_kernel,
        in_specs=[VMEM] * 4,
        out_specs=VMEM,
        out_shape=jax.ShapeDtypeStruct((slices, rank, LANES), f32),
        compiler_params=LIMIT,
        name="near_sum",
    )(keep_in, recv_in, keep_out, recv_out)
    parts = lax.all_to_all(near_sum, "fsdp", 0, 0, tiled=True, axis_index_groups=far)

    outer = pl.pallas_call(
        functools.partial(outer_kernel, in_rank),
        in_specs=[VMEM],
        out_specs=VMEM,
        out_shape=jax.ShapeDtypeStruct((fsdp_count, feature_rows, LANES), f32),
        scratch_shapes=[pltpu.VMEM((rank, LANES), f32)],
        compiler_params=LIMIT,
        name="outer",
    )(parts)
    partials = lax.all_to_all(outer, "fsdp", 0, 0, tiled=True, axis_index_groups=[GATHER_ORDER])

    scores_shape = jax.ShapeDtypeStruct((ex_dev, tests), f32)
    send, scores = pl.pallas_call(
        functools.partial(features_kernel, 1.0 / math.sqrt(LEN), 1.0 / math.sqrt(features)),
        in_specs=[VMEM, VMEM],
        out_specs=[VMEM, VMEM],
        out_shape=[jax.ShapeDtypeStruct((ex_count, 2 * ex_dev, LANES), f32), scores_shape],
        scratch_shapes=[pltpu.VMEM((ex_dev * feature_rows, LANES), f32)],
        compiler_params=LIMIT,
        name="features",
    )(partials, test_features)
    recv = lax.all_to_all(send, "ex", 0, 0, tiled=True, axis_index_groups=[EX_ORDER])
    kernel, scores_t = pl.pallas_call(
        functools.partial(tile_kernel, ex_dev * ex_count),
        in_specs=[VMEM, VMEM],
        out_specs=[VMEM, VMEM],
        out_shape=[
            jax.ShapeDtypeStruct((features // fsdp_count, features // ex_count), f32),
            scores_shape,
        ],
        compiler_params=LIMIT,
        name="tile",
    )(recv, scores)
    return (kernel, scores_t.T)


def solution(mesh):
    in_specs = (P("ex", "fsdp"), P("ex", "fsdp"), P("fsdp", None), P("fsdp", None), P("fsdp", None))
    out_specs = (P("fsdp", "ex"), P("fsdp", "ex"))
    return jax.shard_map(shards, mesh=mesh, in_specs=in_specs, out_specs=out_specs, check_vma=False)
```

```python
import functools
import math

import jax
import jax.numpy as jnp
from jax import lax
from jax.experimental import pallas as pl
from jax.experimental.pallas import tpu as pltpu
from jax.sharding import PartitionSpec as P

LEN = 1024
LANES = 128
EX_ORDER = [10, 5, 12, 9, 14, 3, 0, 8, 13, 2, 15, 6, 11, 1, 4, 7]
GATHER_ORDER = [9, 24, 14, 10, 28, 1, 5, 3, 22, 21, 13, 12, 23, 16, 27, 6, 7, 29, 8, 25, 0, 26, 2, 30, 20, 31, 19, 11, 4, 17, 18, 15]
FAR_ORDER = [1, 6, 5, 4, 7, 0, 2, 3]
Z = 4
LIMIT = pltpu.CompilerParams(vmem_limit_bytes=16 * 2**20)
HIGHEST = lax.Precision.HIGHEST
VMEM = pl.BlockSpec(memory_space=pltpu.VMEM)
HBM = pl.BlockSpec(memory_space=pltpu.HBM)


def nt_dot(a, b, **kw):
    return lax.dot_general(a, b, (((1,), (1,)), ((), ())), preferred_element_type=jnp.float32, **kw)


def block_place(f):
    return f // Z % 2 * 2 + f % 2


def place_order(ex_count):
    own = block_place(lax.axis_index("fsdp"))
    first = 2 - lax.axis_index("ex") % 2
    return own ^ first, own ^ 3, own, own ^ 3 ^ first


def project_kernel(along_rows, ex_count, arg_ref, weights_ref, give_ref, keep_ref):
    for k, place in enumerate(place_order(ex_count)):
        own = pl.ds(pl.multiple_of(place * LEN, LEN), LEN)
        if along_rows:
            proj = nt_dot(weights_ref[...], arg_ref[own, :])
        else:
            proj = jnp.dot(weights_ref[...], arg_ref[:, own], preferred_element_type=jnp.float32)
        out_ref = keep_ref if k >= 2 else give_ref
        for s in range(LEN // LANES):
            out_ref[k % 2, s] = proj[:, s * LANES : (s + 1) * LANES]


def project_rows_kernel(kept, ex_count, arg_hbm, weights_hbm, out_ref, arg, weights, sems):
    copies = [pltpu.make_async_copy(weights_hbm, weights, sems.at[2])]
    for k, place in enumerate(place_order(ex_count)[2 * kept : 2 * kept + 2]):
        own = pl.ds(pl.multiple_of(place * LEN, LEN), LEN)
        copies.append(pltpu.make_async_copy(arg_hbm.at[own, :], arg.at[k], sems.at[k]))
    for copy in copies:
        copy.start()
    copies[0].wait()
    for k in range(2):
        copies[1 + k].wait()
        proj = nt_dot(weights[...], arg[k])
        for s in range(LEN // LANES):
            out_ref[k, s] = proj[:, s * LANES : (s + 1) * LANES]


def block_groups(fsdp_count):
    blocks = range(fsdp_count // Z // 2)
    place = lambda y, z, dy, dz: (2 * y + dy) * Z + 2 * z + dz
    pair, halves = range(2), range(Z // 2)
    near = [[place(y, z, dy, dz) for dy in pair for dz in pair] for y in blocks for z in halves]
    far = [[place(y, z, dy, dz) for y in blocks for z in halves] for dy in pair for dz in pair]
    return near, far


def pair_sum_kernel(keep_ref, recv_ref, keep_next_ref, give_next_ref):
    keep_next_ref[...] = keep_ref[0] + recv_ref[0]
    give_next_ref[...] = keep_ref[1] + recv_ref[1]


def near_sum_kernel(keep_in_ref, recv_in_ref, keep_out_ref, recv_out_ref, sum_ref):
    in_rank = keep_in_ref.shape[1]
    sum_ref[:, :in_rank, :] = keep_in_ref[...] + recv_in_ref[...]
    sum_ref[:, in_rank:, :] = keep_out_ref[...] + recv_out_ref[...]


def outer_kernel(in_rank, parts_ref, out_ref, sum_ref):
    total = parts_ref[0]
    for s in range(1, parts_ref.shape[0]):
        total = total + parts_ref[s]
    sum_ref[...] = total
    out_rank = total.shape[0] - in_rank
    per_row = LANES // out_rank
    rows = in_rank // per_row
    proj_in = jnp.concatenate(
        [sum_ref[pl.ds(a, rows, stride=per_row), :] for a in range(per_row)], axis=0
    )
    proj_out = jnp.concatenate([total[in_rank:]] * per_row, axis=0)
    full = nt_dot(proj_in, proj_out, precision=HIGHEST)
    group = lax.broadcasted_iota(jnp.int32, (rows, LANES), 1) // out_rank
    dense = full[:rows]
    for a in range(1, per_row):
        dense = jnp.where(group == a, full[a * rows : (a + 1) * rows], dense)
    out_ref[...] = jnp.broadcast_to(dense[None], out_ref.shape)


def features_kernel(factor_scale, score_scale, parts_ref, test_ref, send_ref, scores_ref, phi_ref):
    sources, rows, _ = parts_ref.shape
    ex_dev, tests = scores_ref.shape
    weighted = []
    for x in range(ex_dev):
        phi = sum(parts_ref[f] for f in range(sources) if block_place(GATHER_ORDER[f]) == x) * factor_scale
        phi_ref[x * rows : (x + 1) * rows, :] = phi
        acc = jnp.zeros((tests, LANES), jnp.float32)
        for r in range(rows):
            acc = acc + test_ref[:, r * LANES : (r + 1) * LANES] * phi[r : r + 1, :]
        weighted.append(acc)
    me = lax.axis_index("fsdp")
    own = phi_ref[pl.ds(me // 2, ex_dev, stride=rows), :]
    own = jnp.where(me % 2 == 0, own, pltpu.roll(own, LANES // 2, 1))
    for k, r in enumerate(EX_ORDER):
        send_ref[k, :ex_dev, :] = phi_ref[pl.ds(r, ex_dev, stride=rows), :]
        send_ref[k, ex_dev:, :] = own
    ones = jnp.ones((8, LANES), jnp.float32)
    sums = nt_dot(ones, jnp.concatenate(weighted, axis=0), precision=HIGHEST) * score_scale
    for x in range(ex_dev):
        scores_ref[x : x + 1, :] = sums[0:1, x * tests : (x + 1) * tests]


def tile_kernel(ex_all, recv_ref, scores_ref, out_ref, scores_out_ref):
    scores_out_ref[...] = scores_ref[...]
    groups, both, _ = recv_ref.shape
    half = both // 2
    recv = recv_ref[...]
    first = lax.broadcasted_iota(jnp.int32, recv.shape, 1) < half
    cols = jnp.where(first, recv, 0.0).reshape(groups * both, LANES)
    swapped = jnp.concatenate([recv[:, half:], recv[:, :half]], axis=1)
    rows = jnp.where(first, swapped, 0.0).reshape(groups * both, LANES)
    tile = lax.dot_general(
        rows, cols, (((0,), (0,)), ((), ())), preferred_element_type=jnp.float32, precision=HIGHEST
    )
    height = out_ref.shape[0]
    row_start = lax.axis_index("fsdp") * height
    col_start = lax.axis_index("ex") * LANES
    row_index = row_start + lax.broadcasted_iota(jnp.int32, out_ref.shape, 0)
    col_index = col_start + lax.broadcasted_iota(jnp.int32, out_ref.shape, 1)
    eye = jnp.where(row_index == col_index, 1.0, 0.0).astype(jnp.float32)
    out_ref[...] = tile[:height] * (1.0 / ex_all) + eye


def shards(activations, out_grads, in_factor, out_factor, test_features):
    fsdp_count = lax.axis_size("fsdp")
    ex_count = lax.axis_size("ex")
    rows_total, in_width = activations.shape
    out_width = out_grads.shape[1]
    in_rank = in_factor.shape[1]
    out_rank = out_factor.shape[1]
    rank = in_rank + out_rank
    features = in_rank * out_rank
    ex_dev = rows_total // LEN
    tests = test_features.shape[0]
    feature_rows = features // LANES
    f32 = jnp.float32
    near, far = block_groups(fsdp_count)
    slices = len(far[0])

    def swap(value, step):
        pairs = []
        for e in range(ex_count):
            mask = 2 - e % 2 if step == 0 else 1 + e % 2
            for group in near:
                pairs += [(f * ex_count + e, group[b ^ mask] * ex_count + e) for b, f in enumerate(group)]
        return lax.ppermute(value, ("fsdp", "ex"), pairs)

    def project(arg, weights, along_rows, name):
        out_shape = jax.ShapeDtypeStruct((2, slices, weights.shape[0], LANES), f32)
        return pl.pallas_call(
            functools.partial(project_kernel, along_rows, ex_count),
            in_specs=[VMEM] * 2,
            out_specs=[VMEM] * 2,
            out_shape=[out_shape] * 2,
            compiler_params=LIMIT,
            name=name,
        )(arg, weights)

    def project_rows(arg, weights, kept, name):
        return pl.pallas_call(
            functools.partial(project_rows_kernel, kept, ex_count),
            in_specs=[HBM] * 2,
            out_specs=VMEM,
            out_shape=jax.ShapeDtypeStruct((2, slices, weights.shape[0], LANES), f32),
            scratch_shapes=[
                pltpu.VMEM((2, LEN, arg.shape[1]), arg.dtype),
                pltpu.VMEM(weights.shape, weights.dtype),
                pltpu.SemaphoreType.DMA((3,)),
            ],
            compiler_params=pltpu.CompilerParams(vmem_limit_bytes=53 * 2**20 if not kept else 58 * 2**20),
            name=name,
        )(arg, weights)

    def pair_sum(keep, recv):
        out_shape = jax.ShapeDtypeStruct(keep.shape[1:], f32)
        return pl.pallas_call(
            pair_sum_kernel,
            in_specs=[VMEM] * 2,
            out_specs=[VMEM] * 2,
            out_shape=[out_shape] * 2,
            compiler_params=LIMIT,
            name="pair_sum",
        )(keep, recv)

    give_in = project_rows(activations, in_factor.T, 0, "project_in_give")
    give_in, out_grads, activations = lax.optimization_barrier((give_in, out_grads, activations))
    recv_in = swap(give_in, 0)
    keep_in = project_rows(activations, in_factor.T, 1, "project_in_keep")
    keep_in, out_grads = lax.optimization_barrier((keep_in, out_grads))
    give_out, keep_out = project(out_grads.T, out_factor.T, False, "project_out")
    recv_out = swap(give_out, 0)
    keep_in, give_in = pair_sum(keep_in, recv_in)
    recv_in = swap(give_in, 1)
    keep_out, give_out = pair_sum(keep_out, recv_out)
    recv_out = swap(give_out, 1)
    near_sum = pl.pallas_call(
        near_sum_kernel,
        in_specs=[VMEM] * 4,
        out_specs=VMEM,
        out_shape=jax.ShapeDtypeStruct((slices, rank, LANES), f32),
        compiler_params=LIMIT,
        name="near_sum",
    )(keep_in, recv_in, keep_out, recv_out)
    parts = lax.all_to_all(
        near_sum, "fsdp", 0, 0, tiled=True, axis_index_groups=[[group[k] for k in FAR_ORDER] for group in far]
    )

    outer = pl.pallas_call(
        functools.partial(outer_kernel, in_rank),
        in_specs=[VMEM],
        out_specs=VMEM,
        out_shape=jax.ShapeDtypeStruct((fsdp_count, feature_rows, LANES), f32),
        scratch_shapes=[pltpu.VMEM((rank, LANES), f32)],
        compiler_params=LIMIT,
        name="outer",
    )(parts)
    partials = lax.all_to_all(outer, "fsdp", 0, 0, tiled=True, axis_index_groups=[GATHER_ORDER])

    scores_shape = jax.ShapeDtypeStruct((ex_dev, tests), f32)
    send, scores = pl.pallas_call(
        functools.partial(features_kernel, 1.0 / math.sqrt(LEN), 1.0 / math.sqrt(features)),
        in_specs=[VMEM, VMEM],
        out_specs=[VMEM, VMEM],
        out_shape=[jax.ShapeDtypeStruct((ex_count, 2 * ex_dev, LANES), f32), scores_shape],
        scratch_shapes=[pltpu.VMEM((ex_dev * feature_rows, LANES), f32)],
        compiler_params=LIMIT,
        name="features",
    )(partials, test_features)
    recv = lax.all_to_all(send, "ex", 0, 0, tiled=True, axis_index_groups=[EX_ORDER])
    kernel, scores_t = pl.pallas_call(
        functools.partial(tile_kernel, ex_dev * ex_count),
        in_specs=[VMEM, VMEM],
        out_specs=[VMEM, VMEM],
        out_shape=[
            jax.ShapeDtypeStruct((features // fsdp_count, features // ex_count), f32),
            scores_shape,
        ],
        compiler_params=LIMIT,
        name="tile",
    )(recv, scores)
    return (kernel, scores_t.T)


def solution(mesh):
    in_specs = (P("ex", "fsdp"), P("ex", "fsdp"), P("fsdp", None), P("fsdp", None), P("fsdp", None))
    out_specs = (P("fsdp", "ex"), P("fsdp", "ex"))
    return jax.shard_map(shards, mesh=mesh, in_specs=in_specs, out_specs=out_specs, check_vma=False)
```

```python
import functools
import math

import jax
import jax.numpy as jnp
from jax import lax
from jax.experimental import pallas as pl
from jax.experimental.pallas import tpu as pltpu
from jax.sharding import PartitionSpec as P

LEN = 1024
LANES = 128
EX_ORDER = [10, 5, 12, 9, 14, 3, 0, 8, 13, 2, 15, 6, 11, 1, 4, 7]
GATHER_ORDER = [9, 24, 14, 10, 28, 1, 5, 3, 22, 21, 13, 12, 23, 16, 27, 6, 7, 29, 8, 25, 0, 26, 2, 30, 20, 31, 19, 11, 4, 17, 18, 15]
FAR_ORDER = [1, 6, 5, 4, 7, 0, 2, 3]
Z = 4
LIMIT = pltpu.CompilerParams(vmem_limit_bytes=16 * 2**20)
HIGHEST = lax.Precision.HIGHEST
VMEM = pl.BlockSpec(memory_space=pltpu.VMEM)
HBM = pl.BlockSpec(memory_space=pltpu.HBM)


def nt_dot(a, b, **kw):
    return lax.dot_general(a, b, (((1,), (1,)), ((), ())), preferred_element_type=jnp.float32, **kw)


def block_place(f):
    return f // Z % 2 * 2 + f % 2


def place_order(ex_count):
    own = block_place(lax.axis_index("fsdp"))
    first = 1 + lax.axis_index("ex") % 2
    return own ^ first, own ^ 3, own, own ^ 3 ^ first


def project_kernel(along_rows, ex_count, arg_ref, weights_ref, give_ref, keep_ref):
    for k, place in enumerate(place_order(ex_count)):
        own = pl.ds(pl.multiple_of(place * LEN, LEN), LEN)
        if along_rows:
            proj = nt_dot(weights_ref[...], arg_ref[own, :])
        else:
            proj = jnp.dot(weights_ref[...], arg_ref[:, own], preferred_element_type=jnp.float32)
        out_ref = keep_ref if k >= 2 else give_ref
        for s in range(LEN // LANES):
            out_ref[k % 2, s] = proj[:, s * LANES : (s + 1) * LANES]


def project_rows_kernel(kept, ex_count, arg_hbm, weights_hbm, out_ref, arg, weights, sems):
    copies = [pltpu.make_async_copy(weights_hbm, weights, sems.at[2])]
    for k, place in enumerate(place_order(ex_count)[2 * kept : 2 * kept + 2]):
        own = pl.ds(pl.multiple_of(place * LEN, LEN), LEN)
        copies.append(pltpu.make_async_copy(arg_hbm.at[own, :], arg.at[k], sems.at[k]))
    for copy in copies:
        copy.start()
    copies[0].wait()
    for k in range(2):
        copies[1 + k].wait()
        proj = nt_dot(weights[...], arg[k])
        for s in range(LEN // LANES):
            out_ref[k, s] = proj[:, s * LANES : (s + 1) * LANES]


def block_groups(fsdp_count):
    blocks = range(fsdp_count // Z // 2)
    place = lambda y, z, dy, dz: (2 * y + dy) * Z + 2 * z + dz
    pair, halves = range(2), range(Z // 2)
    near = [[place(y, z, dy, dz) for dy in pair for dz in pair] for y in blocks for z in halves]
    far = [[place(y, z, dy, dz) for y in blocks for z in halves] for dy in pair for dz in pair]
    return near, far


def pair_sum_kernel(keep_ref, recv_ref, keep_next_ref, give_next_ref):
    keep_next_ref[...] = keep_ref[0] + recv_ref[0]
    give_next_ref[...] = keep_ref[1] + recv_ref[1]


def near_sum_kernel(keep_in_ref, recv_in_ref, keep_out_ref, recv_out_ref, sum_ref):
    in_rank = keep_in_ref.shape[1]
    sum_ref[:, :in_rank, :] = keep_in_ref[...] + recv_in_ref[...]
    sum_ref[:, in_rank:, :] = keep_out_ref[...] + recv_out_ref[...]


def outer_kernel(in_rank, parts_ref, out_ref, sum_ref):
    total = parts_ref[0]
    for s in range(1, parts_ref.shape[0]):
        total = total + parts_ref[s]
    sum_ref[...] = total
    out_rank = total.shape[0] - in_rank
    per_row = LANES // out_rank
    rows = in_rank // per_row
    proj_in = jnp.concatenate(
        [sum_ref[pl.ds(a, rows, stride=per_row), :] for a in range(per_row)], axis=0
    )
    proj_out = jnp.concatenate([total[in_rank:]] * per_row, axis=0)
    full = nt_dot(proj_in, proj_out, precision=HIGHEST)
    group = lax.broadcasted_iota(jnp.int32, (rows, LANES), 1) // out_rank
    dense = full[:rows]
    for a in range(1, per_row):
        dense = jnp.where(group == a, full[a * rows : (a + 1) * rows], dense)
    out_ref[...] = jnp.broadcast_to(dense[None], out_ref.shape)


def features_kernel(factor_scale, score_scale, parts_ref, test_ref, send_ref, scores_ref, phi_ref):
    sources, rows, _ = parts_ref.shape
    ex_dev, tests = scores_ref.shape
    weighted = []
    for x in range(ex_dev):
        phi = sum(parts_ref[f] for f in range(sources) if block_place(GATHER_ORDER[f]) == x) * factor_scale
        phi_ref[x * rows : (x + 1) * rows, :] = phi
        acc = jnp.zeros((tests, LANES), jnp.float32)
        for r in range(rows):
            acc = acc + test_ref[:, r * LANES : (r + 1) * LANES] * phi[r : r + 1, :]
        weighted.append(acc)
    me = lax.axis_index("fsdp")
    own = phi_ref[pl.ds(me // 2, ex_dev, stride=rows), :]
    own = jnp.where(me % 2 == 0, own, pltpu.roll(own, LANES // 2, 1))
    for k, r in enumerate(EX_ORDER):
        send_ref[k, :ex_dev, :] = phi_ref[pl.ds(r, ex_dev, stride=rows), :]
        send_ref[k, ex_dev:, :] = own
    ones = jnp.ones((8, LANES), jnp.float32)
    sums = nt_dot(ones, jnp.concatenate(weighted, axis=0), precision=HIGHEST) * score_scale
    for x in range(ex_dev):
        scores_ref[x : x + 1, :] = sums[0:1, x * tests : (x + 1) * tests]


def tile_kernel(ex_all, recv_ref, scores_ref, out_ref, scores_out_ref):
    scores_out_ref[...] = scores_ref[...]
    groups, both, _ = recv_ref.shape
    half = both // 2
    recv = recv_ref[...]
    first = lax.broadcasted_iota(jnp.int32, recv.shape, 1) < half
    cols = jnp.where(first, recv, 0.0).reshape(groups * both, LANES)
    swapped = jnp.concatenate([recv[:, half:], recv[:, :half]], axis=1)
    rows = jnp.where(first, swapped, 0.0).reshape(groups * both, LANES)
    tile = lax.dot_general(
        rows, cols, (((0,), (0,)), ((), ())), preferred_element_type=jnp.float32, precision=HIGHEST
    )
    height = out_ref.shape[0]
    row_start = lax.axis_index("fsdp") * height
    col_start = lax.axis_index("ex") * LANES
    row_index = row_start + lax.broadcasted_iota(jnp.int32, out_ref.shape, 0)
    col_index = col_start + lax.broadcasted_iota(jnp.int32, out_ref.shape, 1)
    eye = jnp.where(row_index == col_index, 1.0, 0.0).astype(jnp.float32)
    out_ref[...] = tile[:height] * (1.0 / ex_all) + eye


def shards(activations, out_grads, in_factor, out_factor, test_features):
    fsdp_count = lax.axis_size("fsdp")
    ex_count = lax.axis_size("ex")
    rows_total, in_width = activations.shape
    out_width = out_grads.shape[1]
    in_rank = in_factor.shape[1]
    out_rank = out_factor.shape[1]
    rank = in_rank + out_rank
    features = in_rank * out_rank
    ex_dev = rows_total // LEN
    tests = test_features.shape[0]
    feature_rows = features // LANES
    f32 = jnp.float32
    near, far = block_groups(fsdp_count)
    slices = len(far[0])

    def swap(value, step):
        pairs = []
        for e in range(ex_count):
            mask = 1 + e % 2 if step == 0 else 2 - e % 2
            for group in near:
                pairs += [(f * ex_count + e, group[b ^ mask] * ex_count + e) for b, f in enumerate(group)]
        return lax.ppermute(value, ("fsdp", "ex"), pairs)

    def project(arg, weights, along_rows, name):
        out_shape = jax.ShapeDtypeStruct((2, slices, weights.shape[0], LANES), f32)
        return pl.pallas_call(
            functools.partial(project_kernel, along_rows, ex_count),
            in_specs=[VMEM] * 2,
            out_specs=[VMEM] * 2,
            out_shape=[out_shape] * 2,
            compiler_params=LIMIT,
            name=name,
        )(arg, weights)

    def project_rows(arg, weights, kept, name):
        return pl.pallas_call(
            functools.partial(project_rows_kernel, kept, ex_count),
            in_specs=[HBM] * 2,
            out_specs=VMEM,
            out_shape=jax.ShapeDtypeStruct((2, slices, weights.shape[0], LANES), f32),
            scratch_shapes=[
                pltpu.VMEM((2, LEN, arg.shape[1]), arg.dtype),
                pltpu.VMEM(weights.shape, weights.dtype),
                pltpu.SemaphoreType.DMA((3,)),
            ],
            compiler_params=pltpu.CompilerParams(vmem_limit_bytes=53 * 2**20 if not kept else 58 * 2**20),
            name=name,
        )(arg, weights)

    def pair_sum(keep, recv):
        out_shape = jax.ShapeDtypeStruct(keep.shape[1:], f32)
        return pl.pallas_call(
            pair_sum_kernel,
            in_specs=[VMEM] * 2,
            out_specs=[VMEM] * 2,
            out_shape=[out_shape] * 2,
            compiler_params=LIMIT,
            name="pair_sum",
        )(keep, recv)

    give_in = project_rows(activations, in_factor.T, 0, "project_in_give")
    give_in, out_grads, activations = lax.optimization_barrier((give_in, out_grads, activations))
    recv_in = swap(give_in, 0)
    keep_in = project_rows(activations, in_factor.T, 1, "project_in_keep")
    keep_in, out_grads = lax.optimization_barrier((keep_in, out_grads))
    give_out, keep_out = project(out_grads.T, out_factor.T, False, "project_out")
    recv_out = swap(give_out, 0)
    keep_in, give_in = pair_sum(keep_in, recv_in)
    recv_in = swap(give_in, 1)
    keep_out, give_out = pair_sum(keep_out, recv_out)
    recv_out = swap(give_out, 1)
    near_sum = pl.pallas_call(
        near_sum_kernel,
        in_specs=[VMEM] * 4,
        out_specs=VMEM,
        out_shape=jax.ShapeDtypeStruct((slices, rank, LANES), f32),
        compiler_params=LIMIT,
        name="near_sum",
    )(keep_in, recv_in, keep_out, recv_out)
    parts = lax.all_to_all(
        near_sum, "fsdp", 0, 0, tiled=True, axis_index_groups=[[group[k] for k in FAR_ORDER] for group in far]
    )

    outer = pl.pallas_call(
        functools.partial(outer_kernel, in_rank),
        in_specs=[VMEM],
        out_specs=VMEM,
        out_shape=jax.ShapeDtypeStruct((fsdp_count, feature_rows, LANES), f32),
        scratch_shapes=[pltpu.VMEM((rank, LANES), f32)],
        compiler_params=LIMIT,
        name="outer",
    )(parts)
    partials = lax.all_to_all(outer, "fsdp", 0, 0, tiled=True, axis_index_groups=[GATHER_ORDER])

    scores_shape = jax.ShapeDtypeStruct((ex_dev, tests), f32)
    send, scores = pl.pallas_call(
        functools.partial(features_kernel, 1.0 / math.sqrt(LEN), 1.0 / math.sqrt(features)),
        in_specs=[VMEM, VMEM],
        out_specs=[VMEM, VMEM],
        out_shape=[jax.ShapeDtypeStruct((ex_count, 2 * ex_dev, LANES), f32), scores_shape],
        scratch_shapes=[pltpu.VMEM((ex_dev * feature_rows, LANES), f32)],
        compiler_params=LIMIT,
        name="features",
    )(partials, test_features)
    recv = lax.all_to_all(send, "ex", 0, 0, tiled=True, axis_index_groups=[EX_ORDER])
    kernel, scores_t = pl.pallas_call(
        functools.partial(tile_kernel, ex_dev * ex_count),
        in_specs=[VMEM, VMEM],
        out_specs=[VMEM, VMEM],
        out_shape=[
            jax.ShapeDtypeStruct((features // fsdp_count, features // ex_count), f32),
            scores_shape,
        ],
        compiler_params=LIMIT,
        name="tile",
    )(recv, scores)
    return (kernel, scores_t.T)


def solution(mesh):
    in_specs = (P("ex", "fsdp"), P("ex", "fsdp"), P("fsdp", None), P("fsdp", None), P("fsdp", None))
    out_specs = (P("fsdp", "ex"), P("fsdp", "ex"))
    return jax.shard_map(shards, mesh=mesh, in_specs=in_specs, out_specs=out_specs, check_vma=False)
```
